32 devices in a mesh: tok: 8 (over z, y), exp: 4 (over x, core).
Axes of the slice: x: 2, y: 2, z: 4, core: 2. Of those that a mesh axis runs over, the one named last changes fastest.
Arguments:
- tokens: bfloat16 [12, 8192, 1024], P(None, 'tok'), may hold values from -24 to 24
- slot_params: bfloat16 [1024, 128], P(None, 'exp'), may hold values from -2 to 2
- w_in: bfloat16 [64, 1024, 4096], P('exp', None, 'tok'), may hold values from -0.75 to 0.75
- w_out: bfloat16 [64, 4096, 1024], P('exp', 'tok'), may hold values from -0.1875 to 0.1875
Outputs:
- mixed: bfloat16 [12, 8192, 1024], P(None, 'tok', 'exp')
The draws below stay inside these ranges and needn't reach their ends.
All inputs are finite; a program needn't handle non-finite values.
Results may differ from the reference program's by a relative error of at most 0.0072.
Values may be sent and summed in bfloat16 or wider, within the bound.
A program may use at most 192 MiB of HBM per device.

```python
import math
import jax
import jax.numpy as jnp
from jax import lax

D = 1024
FF = 4096
EXPERTS = 64
SLOTS_PER = 2
SEQS = 12
SLOTS = 128
LEN = 8192


def slot_helper(key):
    raw = jax.random.normal(jax.random.fold_in(key, 11), (D, SLOTS), jnp.float32)
    return jnp.clip(raw, -6.0, 6.0) * (2.0 / math.sqrt(D))


def draw_slot_params(key, part):
    return slot_helper(key).astype(jnp.bfloat16)


def draw_tokens(key, part):
    base = jax.random.fold_in(key, 23)
    values = jnp.clip(jax.random.normal(base, (SEQS, LEN, D), jnp.float32), -6.0, 6.0)
    return values.astype(jnp.bfloat16)


def block_levels(key, dims, cuts, low, largest):
    def one(dim, blocks):
        draws = jax.random.uniform(jax.random.fold_in(jax.random.fold_in(key, 6), dim), (blocks,), jnp.float32, low / len(cuts), largest / len(cuts))
        return jnp.repeat(jnp.exp(draws), dims[dim] // blocks).reshape((-1,) + (1,) * (len(dims) - dim - 1))

    factor_of = one(*cuts[0])
    for cut in cuts[1:]:
        factor_of = factor_of * one(*cut)
    return factor_of


def bell_draw(key, extent, spread, most, pieces=(), dtype=jnp.bfloat16):
    drawn = jax.random.normal(key, extent, jnp.float32) * spread
    if len(pieces) > 0:
        drawn = block_levels(key, extent, pieces, -0.22, 0.18) * drawn
    return jnp.clip(drawn, min=-most, max=most).astype(dtype)


def setup_inputs(seed: int = 0) -> dict:
    arg_keys = jax.random.split(jax.random.key(seed), 5)
    return {
        "tokens": draw_tokens(jax.random.fold_in(arg_keys[4], 71), 0),
        "slot_params": draw_slot_params(jax.random.fold_in(arg_keys[4], 71), 0),
        "w_in": bell_draw(arg_keys[2], (EXPERTS, D, FF), (D // 16) ** -0.5, 0.75, ((0, 4), (2, 8))),
        "w_out": bell_draw(arg_keys[3], (EXPERTS, FF, D), (FF // 4) ** -0.5, 0.1875, ((0, 4), (1, 8))),
    }


def reference(tokens, slot_params, w_in, w_out):
    def per_sequence(seq_tokens):
        logits = jnp.dot(seq_tokens, slot_params, preferred_element_type=jnp.float32)
        dmax = jnp.max(logits, axis=0)
        dexp = jnp.exp(logits - dmax[None, :])
        den = jnp.sum(dexp, axis=0)
        dweight = dexp.astype(jnp.bfloat16)
        slot_sum = jnp.dot(dweight.T, seq_tokens, preferred_element_type=jnp.float32)
        slot_in = (slot_sum / den[:, None]).astype(jnp.bfloat16)
        cmax = jnp.max(logits, axis=1)
        cexp = jnp.exp(logits - cmax[:, None])
        cweight = (cexp / jnp.sum(cexp, axis=1)[:, None]).astype(jnp.bfloat16)
        return slot_in, cweight

    slot_in, cweight = lax.map(per_sequence, tokens)
    grouped = slot_in.reshape(SEQS, EXPERTS, SLOTS_PER, D).transpose(1, 0, 2, 3).reshape(EXPERTS, SEQS * SLOTS_PER, D)

    def per_expert(items):
        expert_in, first, second = items
        hidden = jax.nn.gelu(jnp.dot(expert_in, first, preferred_element_type=jnp.float32), approximate=True).astype(jnp.bfloat16)
        return jnp.dot(hidden, second, preferred_element_type=jnp.float32).astype(jnp.bfloat16)

    outputs = lax.map(per_expert, (grouped, w_in, w_out))
    slot_out = outputs.reshape(EXPERTS, SEQS, SLOTS_PER, D).transpose(1, 0, 2, 3).reshape(SEQS, SLOTS, D)

    def per_combine(items):
        weights, values = items
        return jnp.dot(weights, values, preferred_element_type=jnp.float32).astype(jnp.bfloat16)

    return lax.map(per_combine, (cweight, slot_out))
```

```python
import functools

import jax
import jax.numpy as jnp
from jax import lax
from jax.experimental import pallas as pl
from jax.experimental.pallas import tpu as pltpu
from jax.sharding import PartitionSpec as P

SLOTS_PER = 2
NZ, NY = 4, 2
NT = NZ * NY
NE = 4
NG = 3
TB = 4
LANES = 128
MESH = pl.DeviceIdType.MESH
F32, BF16 = jnp.float32, jnp.bfloat16


def gelu(v):
    return 0.5 * v * (1.0 + jnp.tanh(0.7978845608 * (v + 0.044715 * (v * v * v))))


def main_kernel(
    tok_hbm, prm_ref, win_hbm, wout_hbm, cw_hbm, g_hbm,
    tbuf, prm, prm_t, win, wout, cwbuf, part, psend, st, wrow, yrecv, zsend, zrecv, facc, xs,
    acc, bsend, byrecv, bzsend, bzrecv, fin, g,
    tsem, wsem, cwsem, gsem,
    p_s, p_r, s_s, s_r, y_s, y_r, z_s, z_r, az_s, az_r, ay_s, ay_r,
    by_s, by_r, bz_s, bz_r, c_s, c_r, gl_s, gl_r, gr_s, gr_r, gy_s, gy_r,
):
    seqs, _, width = tok_hbm.shape
    own_w = prm_ref.shape[0]
    pair_rows = acc.shape[1]
    group = seqs // NG
    span = pair_rows // NG
    feat = g.shape[3]
    tiles = width // LANES
    packs = own_w // 8
    t = lax.axis_index("tok")
    e = lax.axis_index("exp")
    z, y = t // NY, t % NY
    oy = 1 - y
    me = y * NZ + z

    def remote(src, dst, ssem, rsem, tok, exp):
        return pltpu.make_async_remote_copy(
            src_ref=src, dst_ref=dst, send_sem=ssem, recv_sem=rsem,
            device_id={"tok": tok, "exp": exp}, device_id_type=MESH)

    def zpeer(d):
        return lax.rem(z + d, NZ)

    def zfrom(d):
        return lax.rem(z + NZ - d, NZ)

    def tok_copy(s):
        slot = lax.rem(s, TB)
        return pltpu.make_async_copy(tok_hbm.at[s], tbuf.at[slot], tsem.at[slot])

    def win_copy(p):
        return pltpu.make_async_copy(win_hbm.at[pl.ds(2 * p, 2)], win.at[pl.ds(2 * p, 2)], wsem.at[p])

    def wout_copy(h):
        half = wout.shape[0] // 2
        return pltpu.make_async_copy(wout_hbm.at[pl.ds(h * half, half)], wout.at[pl.ds(h * half, half)], wsem.at[NT + h])

    def cw_copy(i):
        return pltpu.make_async_copy(cwbuf.at[pl.ds(i * group, group)], cw_hbm.at[pl.ds(i * group, group)], cwsem.at[i])

    for s in range(TB - 1):
        tok_copy(s).start()

    barrier = pltpu.get_barrier_semaphore()
    for d in range(1, NT):
        pl.semaphore_signal(barrier, inc=1, device_id={"tok": lax.rem(t + d, NT), "exp": e}, device_id_type=MESH)
    for d in range(1, NE):
        pl.semaphore_signal(barrier, inc=1, device_id={"tok": t, "exp": lax.rem(e + d, NE)}, device_id_type=MESH)

    for i in range(NG):
        st[i, me] = jnp.ones((8, LANES), F32)
    lane = lax.broadcasted_iota(jnp.int32, (8, LANES), 1)

    def own_logits(s):
        return lax.dot_general(prm_ref[...], tbuf[lax.rem(s, TB)], (((1,), (1,)), ((), ())), preferred_element_type=F32)

    def emit(s, own):
        gi, in_group = s // group, lax.rem(s, group)
        peak = jnp.max(own, axis=1, keepdims=True)
        dx = jnp.exp(own - peak)
        den = jnp.sum(dx, axis=1, keepdims=True)
        ssum = jnp.dot(dx.astype(BF16), tbuf[lax.rem(s, TB)], preferred_element_type=F32)
        scaled = ssum / den
        for k in range(tiles):
            part[gi, k, pl.ds(in_group, own_w, stride=group), :] = scaled[:, k * LANES:(k + 1) * LANES]
        stats = st[gi, me]
        for a in range(packs):
            at = a * group + in_group
            stats = jnp.where(lane == at, peak[8 * a:8 * a + 8], jnp.where(lane == at + 64, den[8 * a:8 * a + 8], stats))
        st[gi, me] = stats

    def dispatch(s, own):
        @pl.when(s + TB - 1 < seqs)
        def _():
            tok_copy(s + TB - 1).start()

        @pl.when(s >= group)
        def _():
            win_copy(s - group).start()

        tok_copy(s + 1).wait()
        later = own_logits(s + 1)
        emit(s, own)
        return later

    y_tok = z * NY + oy

    def st_copy(i, d):
        return remote(st.at[i, me], st.at[i, me], s_s.at[i, d - 1], s_r.at[i, d - 1], lax.rem(t + d, NT), e)

    def y_copy(i):
        return remote(psend.at[i], yrecv.at[i], y_s.at[i], y_r.at[i], y_tok, e)

    def z_copy(i, d):
        zz = zpeer(d)
        return remote(zsend.at[i, zz], zrecv.at[i, d - 1], z_s.at[i, d - 1], z_r.at[i, d - 1], zz * NY + y, e)

    def az_copy(i, d):
        return remote(xs.at[i, me], xs.at[i, me], az_s.at[i, d - 1], az_r.at[i, d - 1], zpeer(d) * NY + y, e)

    def ay_copy(i, d):
        got = y * NZ + zfrom(d)
        return remote(xs.at[i, got], xs.at[i, got], ay_s.at[i, d], ay_r.at[i, d], y_tok, e)

    def pair_slice(p):
        return pl.ds(pl.multiple_of(p * span, span), span)

    def send_partial(i):
        for d in range(1, NT):
            st_copy(i, d).start()
        for zz in range(NZ):
            rows = pair_slice(oy * NZ + zz)
            for k in range(tiles):
                psend[i, zz, :, k * LANES:(k + 1) * LANES] = part[i, k, rows, :].astype(BF16)
        y_copy(i).start()

    def reduce_y(i):
        for d in range(1, NT):
            st_copy(i, d).wait()
        peaks = [st[i, r] for r in range(NT)]
        top = functools.reduce(jnp.maximum, peaks)
        total = jnp.zeros_like(top)
        for r in range(NT):
            total += pltpu.roll(peaks[r], 64, 1) * jnp.exp(peaks[r] - top)
        for n, r in enumerate((me, oy * NZ + z)):
            mine = st[i, r]
            w = pltpu.roll(mine, 64, 1) * jnp.exp(mine - top) / total
            for a in range(packs):
                for q in range(group):
                    at = a * group + q
                    wrow[n, pl.ds(8 * a * group + q, 8, stride=group), :] = jnp.broadcast_to(w[:, at:at + 1], (8, LANES))
        y_copy(i).wait()
        for d in (1, 2, 3, 0):
            zz = zpeer(d)
            rows = pair_slice(y * NZ + zz)
            w0, w1 = wrow[0, rows, :], wrow[1, rows, :]
            for k in range(tiles):
                cols = slice(k * LANES, (k + 1) * LANES)
                both = part[i, k, rows, :] * w0 + yrecv[i, zz, :, cols].astype(F32) * w1
                if d:
                    zsend[i, zz, :, cols] = both.astype(BF16)
                else:
                    facc[i, :, cols] = both
            if d:
                z_copy(i, d).start()

    def finish_z(i):
        for d in range(1, NZ):
            z_copy(i, d).wait()
        xs[i, me] = (facc[i] + zrecv[i, 0].astype(F32) + zrecv[i, 1].astype(F32) + zrecv[i, 2].astype(F32)).astype(BF16)
        ay_copy(i, 0).start()
        for d in range(1, NZ):
            az_copy(i, d).start()

    def forward(i):
        for d in range(1, NZ):
            az_copy(i, d).wait_recv()
            ay_copy(i, d).start()

    own_rows = pl.ds(pl.multiple_of(e * own_w, own_w), own_w)

    def p_copy(d):
        return remote(prm_ref, prm.at[own_rows], p_s.at[d - 1], p_r.at[d - 1], t, lax.rem(e + d, NE))

    def weigh(c, carry):
        @pl.when(c + TB - 1 < seqs)
        def _():
            tok_copy(c + TB - 1).start()

        tok_copy(c).wait()
        logits = jnp.dot(tbuf[lax.rem(c, TB)], prm_t[...], preferred_element_type=F32)
        ex = jnp.exp(logits - jnp.max(logits, axis=1, keepdims=True))
        cwbuf[c] = (ex / jnp.sum(ex, axis=1, keepdims=True)).astype(BF16)

        @pl.when(lax.rem(c, group) == group - 1)
        def _():
            cw_copy(c // group).start()

        return carry

    def weights(a, b):
        lax.fori_loop(a, b, weigh, 0)

    tok_copy(0).wait()
    own = own_logits(0)
    own = lax.fori_loop(0, group, dispatch, own)
    pl.semaphore_wait(barrier, NT + NE - 2)
    send_partial(0)
    for d in range(1, NE):
        p_copy(d).start()
    prm[own_rows, :] = prm_ref[...]
    own = lax.fori_loop(group, 2 * group, dispatch, own)
    send_partial(1)
    reduce_y(0)
    own = lax.fori_loop(2 * group, seqs - 1, dispatch, own)
    emit(seqs - 1, own)
    send_partial(2)
    win_copy(NT - 1).start()
    for h in range(2):
        wout_copy(h).start()
    for s in range(TB - 1):
        tok_copy(s).start()
    finish_z(0)
    reduce_y(1)
    for d in range(1, NE):
        p_copy(d).wait()
    prm_t[...] = prm[...].astype(F32).T.astype(BF16)
    weights(0, 2)
    reduce_y(2)
    forward(0)
    finish_z(1)
    weights(2, 4)
    finish_z(2)
    forward(1)
    for p in range(NT):
        win_copy(p).wait()
    for h in range(2):
        wout_copy(h).wait()
    ay_copy(0, 0).wait_recv()
    for d in range(1, NZ):
        ay_copy(0, d).wait_recv()

    upper = lax.rem(lax.broadcasted_iota(jnp.int32, (pair_rows, 1), 0), span) < span // 2

    def by_copy(d):
        return remote(bsend.at[d], byrecv.at[d], by_s.at[d], by_r.at[d], y_tok, e)

    def bz_copy(d):
        return remote(bzsend.at[d - 1], bzrecv.at[d - 1], bz_s.at[d - 1], bz_r.at[d - 1], zfrom(d) * NY + y, e)

    def expert_pair(i, carry):
        d = jnp.where(i < 2, 0, jnp.where(i < 4, 1, 2 + lax.rem(i, 2)))
        other = jnp.logical_or(i == 1, jnp.logical_and(i >= 3, i < 6))
        p = jnp.where(other, oy, y) * NZ + zfrom(d)

        @pl.when(i == 1)
        def _():
            weights(4, 5)

        @pl.when(i == 2)
        def _():
            forward(2)

        @pl.when(other)
        def _():
            for n in range(1, NG):
                ay_copy(n, d).wait_recv()

        x = jnp.concatenate([xs[n, p] for n in range(NG)], axis=0)
        h0 = jnp.dot(x, win[2 * p], preferred_element_type=F32)
        h1 = jnp.dot(x, win[2 * p + 1], preferred_element_type=F32)
        hid = gelu(jnp.where(upper, h0, h1))
        zero = jnp.zeros_like(hid)
        u0 = jnp.where(upper, hid, zero).astype(BF16)
        u1 = jnp.where(upper, zero, hid).astype(BF16)
        out = (jnp.dot(u0, wout[2 * p], preferred_element_type=F32)
               + jnp.dot(u1, wout[2 * p + 1], preferred_element_type=F32))

        @pl.when(other)
        def _():
            bsend[d] = out.astype(BF16)
            by_copy(d).start()

        @pl.when(jnp.logical_not(other))
        def _():
            acc[d] = out

        return carry

    lax.fori_loop(0, NT, expert_pair, 0)

    def pass_on(d):
        by_copy(d).wait()
        bzsend[d - 1] = (acc[d] + byrecv[d].astype(F32)).astype(BF16)
        bz_copy(d).start()

    pass_on(1)
    weights(5, 6)
    pass_on(2)
    weights(6, 8)
    pass_on(3)
    by_copy(0).wait()
    acc[0] += byrecv[0].astype(F32)
    weights(8, 10)
    for d in range(1, NZ):
        bz_copy(d).wait()
    done = (acc[0] + bzrecv[0].astype(F32) + bzrecv[1].astype(F32) + bzrecv[2].astype(F32)).astype(BF16)
    for k in range(NE):
        fin[k] = done[:, k * feat:(k + 1) * feat]

    def c_copy(d):
        to = lax.rem(e + d, NE)
        return remote(fin.at[to], g.at[e, me], c_s.at[d - 1], c_r.at[d - 1], t, to)

    for d in range(1, NE):
        c_copy(d).start()
    g[e, me] = fin[e]
    weights(10, 12)
    for d in range(1, NE):
        c_copy(d).wait()
    for n in range(NG):
        for d in range(1, NZ):
            az_copy(n, d).wait_send()
        for d in range(NZ):
            ay_copy(n, d).wait_send()

    def block(zz):
        return g.at[:, y * NZ + zz]

    def hop(zz, sems, n, step):
        to = jnp.clip(z + step, 0, NZ - 1) * NY + y
        return remote(block(zz), block(zz), sems[0].at[n], sems[1].at[n], to, e)

    def cross(zz, n):
        return remote(block(zz), block(zz), gy_s.at[n], gy_r.at[n], y_tok, e)

    ways = ((1, (gr_s, gr_r), 0), (-1, (gl_s, gl_r), NZ - 1))
    for step, sems, off in ways:
        @pl.when(z != NZ - 1 if step == 1 else z != 0)
        def _():
            hop(z, sems, 0, step).start()
    cross(z, 0).start()
    for n in range(1, NZ):
        for step, sems, off in ways:
            zz = z - step * n
            inside = zz >= 0 if step == 1 else zz < NZ
            at = jnp.clip(zz, 0, NZ - 1)
            more = jnp.logical_and(inside, z != NZ - 1 if step == 1 else z != 0)

            @pl.when(inside)
            def _():
                hop(at, sems, n - 1, -step).wait_recv()
                cross(at, off + n).start()

            if n < NZ - 1:
                @pl.when(more)
                def _():
                    hop(at, sems, n, step).start()
    for step, sems, off in ways:
        @pl.when(z != NZ - 1 if step == 1 else z != 0)
        def _():
            hop(z, sems, 0, step).wait_send()
    cross(z, 0).wait()
    for n in range(1, NZ):
        for step, sems, off in ways:
            zz = z - step * n
            inside = zz >= 0 if step == 1 else zz < NZ
            at = jnp.clip(zz, 0, NZ - 1)
            more = jnp.logical_and(inside, z != NZ - 1 if step == 1 else z != 0)

            @pl.when(inside)
            def _():
                cross(at, off + n).wait()

            if n < NZ - 1:
                @pl.when(more)
                def _():
                    hop(at, sems, n, step).wait_send()
    out = pltpu.make_async_copy(g, g_hbm, gsem)
    out.start()
    for i in range(NG):
        cw_copy(i).wait()
    out.wait()


def combine_kernel(cw_hbm, g_ref, o_hbm, cw, vals, o, csem, osem):
    seqs, length, slots = cw.shape
    blocks, _, feat = g_ref.shape
    size = seqs // NG
    span = g_ref.shape[1] // NG

    def cw_in(i):
        return pltpu.make_async_copy(cw_hbm.at[pl.ds(i * size, size)], cw.at[pl.ds(i * size, size)], csem.at[i])

    def out(i):
        return pltpu.make_async_copy(o.at[pl.ds(i * size, size)], o_hbm.at[pl.ds(i * size, size)], osem.at[i])

    for i in range(NG):
        cw_in(i).start()
    row = lax.broadcasted_iota(jnp.int32, (blocks * span, blocks * span), 0)
    col = lax.broadcasted_iota(jnp.int32, (blocks * span, blocks * span), 1)
    order = jnp.where(col == lax.rem(row, slots) * size + row // slots, 1.0, 0.0).astype(BF16)
    for i in range(NG):
        part = g_ref[:, i * span:(i + 1) * span, :].reshape(blocks * span, feat)
        vals[i] = jnp.dot(order, part, preferred_element_type=F32).astype(BF16)
    for i in range(NG):
        cw_in(i).wait()
        for q in range(size):
            s = i * size + q
            o[s] = jnp.dot(cw[s], vals[i, q * slots:(q + 1) * slots], preferred_element_type=F32).astype(BF16)
        out(i).start()
    for i in range(NG):
        out(i).wait()


def fused(tokens, slot_params, w_in, w_out):
    seqs, length, width = tokens.shape
    own_w = slot_params.shape[1]
    slots = own_w * NE
    experts, _, ff = w_in.shape
    rows = seqs * own_w
    pair_rows = rows // NT
    own_rows = rows // NG
    span = own_rows // NT
    feat = width // NE
    tiles = width // LANES
    dma = pltpu.SemaphoreType.DMA
    any_spec = pl.BlockSpec(memory_space=pl.ANY)
    cw, g = pl.pallas_call(
        main_kernel,
        out_shape=(jax.ShapeDtypeStruct((seqs, length, slots), BF16),
                   jax.ShapeDtypeStruct((NE, NT, pair_rows, feat), BF16)),
        in_specs=[any_spec, pl.BlockSpec(memory_space=pltpu.VMEM), any_spec, any_spec],
        out_specs=(any_spec, any_spec),
        scratch_shapes=[
            pltpu.VMEM((TB, length, width), BF16),
            pltpu.VMEM((slots, width), BF16),
            pltpu.VMEM((width, slots), BF16),
            pltpu.VMEM((experts, width, ff), BF16),
            pltpu.VMEM((experts, ff, width), BF16),
            pltpu.VMEM((seqs, length, slots), BF16),
            pltpu.VMEM((NG, tiles, own_rows, LANES), F32),
            pltpu.VMEM((NG, NZ, span, width), BF16),
            pltpu.VMEM((NG, NT, 8, LANES), F32),
            pltpu.VMEM((2, own_rows, LANES), F32),
            pltpu.VMEM((NG, NZ, span, width), BF16),
            pltpu.VMEM((NG, NZ, span, width), BF16),
            pltpu.VMEM((NG, NZ - 1, span, width), BF16),
            pltpu.VMEM((NG, span, width), F32),
            pltpu.VMEM((NG, NT, span, width), BF16),
            pltpu.VMEM((NZ, pair_rows, width), F32),
            pltpu.VMEM((NZ, pair_rows, width), BF16),
            pltpu.VMEM((NZ, pair_rows, width), BF16),
            pltpu.VMEM((NZ - 1, pair_rows, width), BF16),
            pltpu.VMEM((NZ - 1, pair_rows, width), BF16),
            pltpu.VMEM((NE, pair_rows, feat), BF16),
            pltpu.VMEM((NE, NT, pair_rows, feat), BF16),
            dma((TB,)), dma((NT + 2,)), dma((NG,)), dma,
            dma((NE - 1,)), dma((NE - 1,)),
            dma((NG, NT - 1)), dma((NG, NT - 1)),
            dma((NG,)), dma((NG,)),
            dma((NG, NZ - 1)), dma((NG, NZ - 1)),
            dma((NG, NZ - 1)), dma((NG, NZ - 1)),
            dma((NG, NZ)), dma((NG, NZ)),
            dma((NZ,)), dma((NZ,)),
            dma((NZ - 1,)), dma((NZ - 1,)),
            dma((NE - 1,)), dma((NE - 1,)),
            dma((NZ - 1,)), dma((NZ - 1,)),
            dma((NZ - 1,)), dma((NZ - 1,)),
            dma((2 * NZ - 1,)), dma((2 * NZ - 1,)),
        ],
        compiler_params=pltpu.CompilerParams(collective_id=0, has_side_effects=True, vmem_limit_bytes=60 << 20),
        name="dispatch_experts",
    )(tokens, slot_params.T, w_in, w_out)
    return pl.pallas_call(
        combine_kernel,
        out_shape=jax.ShapeDtypeStruct((seqs, length, feat), BF16),
        in_specs=[any_spec, pl.BlockSpec(memory_space=pltpu.VMEM)],
        out_specs=any_spec,
        scratch_shapes=[
            pltpu.VMEM((seqs, length, slots), BF16),
            pltpu.VMEM((NG, NE * NT * span, feat), BF16),
            pltpu.VMEM((seqs, length, feat), BF16),
            dma((NG,)), dma((NG,)),
        ],
        compiler_params=pltpu.CompilerParams(vmem_limit_bytes=60 << 20),
        name="combine",
    )(cw, g.reshape(NE * NT, pair_rows, feat))


def shards(tokens, slot_params, w_in, w_out):
    own_width = slot_params.shape[1]
    own_logits = jnp.einsum("std,dj->sjt", tokens, slot_params, preferred_element_type=jnp.float32)
    all_logits = lax.all_gather(own_logits, "exp", axis=1, tiled=True)
    local_max = jnp.max(own_logits, axis=2)
    slot_peak = lax.pmax(local_max, "tok")
    dexp = jnp.exp(own_logits - slot_peak[:, :, None])
    local_den = jnp.sum(dexp, axis=2)
    dweight = dexp.astype(jnp.bfloat16)
    local_sum = jnp.einsum("sjt,std->sjd", dweight, tokens, preferred_element_type=jnp.float32)
    slot_sum, slot_den = lax.psum((local_sum, local_den), "tok")
    slot_in = (slot_sum / slot_den[:, :, None]).astype(jnp.bfloat16)
    seq_count = tokens.shape[0]
    local_experts = w_in.shape[0]
    width = tokens.shape[2]
    grouped = slot_in.reshape(seq_count, local_experts, SLOTS_PER, width)
    hidden = jax.nn.gelu(
        jnp.einsum("sepd,edf->sepf", grouped, w_in, preferred_element_type=jnp.float32),
        approximate=True,
    ).astype(jnp.bfloat16)
    partial_out = jnp.einsum("sepf,efd->sepd", hidden, w_out, preferred_element_type=jnp.float32)
    partial_out = partial_out.reshape(seq_count, own_width, width)
    summed = lax.psum(partial_out, "tok").astype(jnp.bfloat16)
    slot_out = lax.all_to_all(summed, "exp", split_axis=2, concat_axis=1, tiled=True)
    comb_max = jnp.max(all_logits, axis=1)
    cexp = jnp.exp(all_logits - comb_max[:, None, :])
    cweight = (cexp / jnp.sum(cexp, axis=1)[:, None, :]).astype(jnp.bfloat16)
    mixed = jnp.einsum("sjt,sjd->std", cweight, slot_out, preferred_element_type=jnp.float32)
    return mixed.astype(jnp.bfloat16)


def solution(mesh):
    quick = mesh.shape["tok"] == NT and mesh.shape["exp"] == NE
    return jax.shard_map(
        fused if quick else shards,
        mesh=mesh,
        in_specs=(
            P(None, "tok", None),
            P(None, "exp"),
            P("exp", None, "tok"),
            P("exp", "tok", None),
        ),
        out_specs=P(None, "tok", "exp"),
        check_vma=False,
    )
```

```python
import functools

import jax
import jax.numpy as jnp
from jax import lax
from jax.experimental import pallas as pl
from jax.experimental.pallas import tpu as pltpu
from jax.sharding import PartitionSpec as P

SLOTS_PER = 2
NZ, NY = 4, 2
NT = NZ * NY
NE = 4
NG = 3
TB = 4
LANES = 128
MESH = pl.DeviceIdType.MESH
F32, BF16 = jnp.float32, jnp.bfloat16


def gelu(v):
    return 0.5 * v * (1.0 + jnp.tanh(0.7978845608 * (v + 0.044715 * (v * v * v))))


def main_kernel(
    tok_hbm, prm_ref, win_hbm, wout_hbm, cw_hbm, g_hbm,
    tbuf, prm, prm_t, win, wout, cwbuf, part, psend, st, wrow, yrecv, zsend, zrecv, facc, xs,
    acc, bsend, byrecv, bzsend, bzrecv, fin, g,
    tsem, wsem, cwsem, gsem,
    p_s, p_r, t_s, t_r, s_s, s_r, y_s, y_r, z_s, z_r, az_s, az_r, ay_s, ay_r,
    by_s, by_r, bz_s, bz_r, c_s, c_r,
):
    seqs, length, width = tok_hbm.shape
    half = length // 2
    own_w = prm_ref.shape[0]
    pair_rows = acc.shape[1]
    group = seqs // NG
    span = pair_rows // NG
    feat = g.shape[3]
    tiles = width // LANES
    packs = own_w // 8
    t = lax.axis_index("tok")
    e = lax.axis_index("exp")
    z, y = t // NY, t % NY
    oy = 1 - y
    me = y * NZ + z
    side, core = e // 2, lax.rem(e, 2)
    half_rows = pl.ds(pl.multiple_of(core * half, half), half)
    cross_e = (lax.rem(e + 2, NE), e + 1 - 2 * core, lax.rem(e + 2, NE) + 1 - 2 * core)
    g_at = 2 * core + side

    def remote(src, dst, ssem, rsem, tok, exp):
        return pltpu.make_async_remote_copy(
            src_ref=src, dst_ref=dst, send_sem=ssem, recv_sem=rsem,
            device_id={"tok": tok, "exp": exp}, device_id_type=MESH)

    def zpeer(d):
        return lax.rem(z + d, NZ)

    def zfrom(d):
        return lax.rem(z + NZ - d, NZ)

    def tok_copy(s):
        slot = lax.rem(s, TB)
        return pltpu.make_async_copy(tok_hbm.at[s], tbuf.at[slot], tsem.at[slot])

    def win_copy(p):
        return pltpu.make_async_copy(win_hbm.at[pl.ds(2 * p, 2)], win.at[pl.ds(2 * p, 2)], wsem.at[p])

    def wout_copy(p):
        return pltpu.make_async_copy(wout_hbm.at[pl.ds(2 * p, 2)], wout.at[pl.ds(2 * p, 2)], wsem.at[NT + p])

    def load_weights(n):
        @pl.when(n < NT)
        def _():
            win_copy(n).start()

        @pl.when(n >= NT)
        def _():
            wout_copy(n - NT).start()

    def cw_copy(i):
        at = pl.ds(i * group, group)
        return pltpu.make_async_copy(cwbuf.at[at], cw_hbm.at[at, half_rows], cwsem.at[i])

    def cw_send(i):
        at = pl.ds(i * group, group)
        return remote(cwbuf.at[at], cw_hbm.at[at, half_rows], t_s.at[i], t_r.at[i], t, e + 1 - 2 * core)

    def half_copy(n):
        slot = lax.rem(n, TB)
        return pltpu.make_async_copy(tok_hbm.at[n, half_rows], tbuf.at[slot, pl.ds(0, half)], tsem.at[slot])

    for s in range(TB - 1):
        tok_copy(s).start()

    barrier = pltpu.get_barrier_semaphore()
    for d in range(1, NT):
        pl.semaphore_signal(barrier, inc=1, device_id={"tok": lax.rem(t + d, NT), "exp": e}, device_id_type=MESH)
    for d in range(1, NE):
        pl.semaphore_signal(barrier, inc=1, device_id={"tok": t, "exp": lax.rem(e + d, NE)}, device_id_type=MESH)

    for i in range(NG):
        st[i, me] = jnp.ones((8, LANES), F32)
    lane = lax.broadcasted_iota(jnp.int32, (8, LANES), 1)

    def own_logits(s):
        return lax.dot_general(prm_ref[...], tbuf[lax.rem(s, TB)], (((1,), (1,)), ((), ())), preferred_element_type=F32)

    def emit(s, own):
        gi, in_group = s // group, lax.rem(s, group)
        peak = jnp.max(own, axis=1, keepdims=True)
        dx = jnp.exp(own - peak)
        den = jnp.sum(dx, axis=1, keepdims=True)
        ssum = jnp.dot(dx.astype(BF16), tbuf[lax.rem(s, TB)], preferred_element_type=F32)
        scaled = ssum / den
        for k in range(tiles):
            part[gi, k, pl.ds(in_group, own_w, stride=group), :] = scaled[:, k * LANES:(k + 1) * LANES]
        stats = st[gi, me]
        for a in range(packs):
            at = a * group + in_group
            stats = jnp.where(lane == at, peak[8 * a:8 * a + 8], jnp.where(lane == at + 64, den[8 * a:8 * a + 8], stats))
        st[gi, me] = stats

    def dispatch(s, own):
        @pl.when(s + TB - 1 < seqs)
        def _():
            tok_copy(s + TB - 1).start()

        @pl.when(s + TB - 1 >= seqs)
        def _():
            half_copy(s + TB - 1 - seqs).start()

        @pl.when(jnp.logical_and(s < NT, lax.rem(s, 2) == 1))
        def _():
            win_copy(s // 2).start()

        @pl.when(s >= NT)
        def _():
            win_copy(s - group).start()

        tok_copy(s + 1).wait()
        later = own_logits(s + 1)
        emit(s, own)
        return later

    y_tok = z * NY + oy

    def st_copy(i, d):
        return remote(st.at[i, me], st.at[i, me], s_s.at[i, d - 1], s_r.at[i, d - 1], lax.rem(t + d, NT), e)

    def y_copy(i):
        return remote(psend.at[i], yrecv.at[i], y_s.at[i], y_r.at[i], y_tok, e)

    def z_copy(i, d):
        zz = zpeer(d)
        return remote(zsend.at[i, zz], zrecv.at[i, d - 1], z_s.at[i, d - 1], z_r.at[i, d - 1], zz * NY + y, e)

    def az_copy(i, d):
        return remote(xs.at[i, me], xs.at[i, me], az_s.at[i, d - 1], az_r.at[i, d - 1], zpeer(d) * NY + y, e)

    def ay_copy(i, d):
        got = y * NZ + zfrom(d)
        return remote(xs.at[i, got], xs.at[i, got], ay_s.at[i, d], ay_r.at[i, d], y_tok, e)

    def pair_slice(p):
        return pl.ds(pl.multiple_of(p * span, span), span)

    def send_partial(i):
        for d in range(1, NT):
            st_copy(i, d).start()
        for zz in range(NZ):
            rows = pair_slice(oy * NZ + zz)
            for k in range(tiles):
                psend[i, zz, :, k * LANES:(k + 1) * LANES] = part[i, k, rows, :].astype(BF16)
        y_copy(i).start()

    def reduce_y(i):
        for d in range(1, NT):
            st_copy(i, d).wait()
        peaks = [st[i, r] for r in range(NT)]
        top = functools.reduce(jnp.maximum, peaks)
        total = jnp.zeros_like(top)
        for r in range(NT):
            total += pltpu.roll(peaks[r], 64, 1) * jnp.exp(peaks[r] - top)
        for n, r in enumerate((me, oy * NZ + z)):
            mine = st[i, r]
            w = pltpu.roll(mine, 64, 1) * jnp.exp(mine - top) / total
            for a in range(packs):
                for q in range(group):
                    at = a * group + q
                    wrow[n, pl.ds(8 * a * group + q, 8, stride=group), :] = jnp.broadcast_to(w[:, at:at + 1], (8, LANES))
        y_copy(i).wait()
        for d in (1, 2, 3, 0):
            zz = zpeer(d)
            rows = pair_slice(y * NZ + zz)
            w0, w1 = wrow[0, rows, :], wrow[1, rows, :]
            for k in range(tiles):
                cols = slice(k * LANES, (k + 1) * LANES)
                both = part[i, k, rows, :] * w0 + yrecv[i, zz, :, cols].astype(F32) * w1
                if d:
                    zsend[i, zz, :, cols] = both.astype(BF16)
                else:
                    facc[i, :, cols] = both
            if d:
                z_copy(i, d).start()

    def finish_z(i):
        for d in range(1, NZ):
            z_copy(i, d).wait()
        xs[i, me] = (facc[i] + zrecv[i, 0].astype(F32) + zrecv[i, 1].astype(F32) + zrecv[i, 2].astype(F32)).astype(BF16)
        ay_copy(i, 0).start()
        for d in range(1, NZ):
            az_copy(i, d).start()

    def forward(i):
        for d in range(1, NZ):
            az_copy(i, d).wait_recv()
            ay_copy(i, d).start()

    own_rows = pl.ds(pl.multiple_of(e * own_w, own_w), own_w)

    def p_copy(n):
        return remote(prm_ref, prm.at[own_rows], p_s.at[n], p_r.at[n], t, cross_e[n])

    def weigh(c, carry):
        early = seqs - 1 - group

        @pl.when(c + TB - 1 < seqs)
        def _():
            half_copy(c + TB - 1).start()

        @pl.when(2 * c < 2 * NT - early)
        def _():
            load_weights(2 * c + early)

            @pl.when(2 * c + 1 < 2 * NT - early)
            def _():
                load_weights(2 * c + 1 + early)

        half_copy(c).wait()
        logits = jnp.dot(tbuf[lax.rem(c, TB), 0:half, :], prm_t[...], preferred_element_type=F32)
        ex = jnp.exp(logits - jnp.max(logits, axis=1, keepdims=True))
        cwbuf[c] = (ex / jnp.sum(ex, axis=1, keepdims=True)).astype(BF16)

        @pl.when(lax.rem(c, group) == group - 1)
        def _():
            cw_copy(c // group).start()
            cw_send(c // group).start()

        return carry

    def weights(a, b):
        lax.fori_loop(a, b, weigh, 0)

    def run(a, b, logits):
        return lax.fori_loop(a, b, dispatch, logits)

    tok_copy(0).wait()
    own = own_logits(0)
    own = run(0, 4, own)
    pl.semaphore_wait(barrier, NT + NE - 2)
    send_partial(0)
    for n in range(NE - 1):
        p_copy(n).start()
    prm[own_rows, :] = prm_ref[...]
    own = run(4, 8, own)
    send_partial(1)
    reduce_y(0)
    own = run(8, 11, own)
    emit(seqs - 1, own)
    send_partial(2)
    half_copy(2).start()
    reduce_y(1)
    for n in range(NE - 1):
        p_copy(n).wait()
    prm_t[...] = prm[...].astype(F32).T.astype(BF16)
    weights(0, 2)
    finish_z(0)
    weights(2, 4)
    reduce_y(2)
    finish_z(1)
    weights(4, 6)
    forward(0)
    weights(6, 9)
    finish_z(2)
    for p in range(NT):
        win_copy(p).wait()
    for p in range(NT):
        wout_copy(p).wait()
    ay_copy(0, 0).wait_recv()
    for d in range(1, NZ):
        ay_copy(0, d).wait_recv()

    upper = lax.rem(lax.broadcasted_iota(jnp.int32, (pair_rows, 1), 0), span) < span // 2

    def by_copy(d):
        return remote(bsend.at[d], byrecv.at[d], by_s.at[d], by_r.at[d], y_tok, e)

    def bz_copy(d):
        return remote(bzsend.at[d - 1], bzrecv.at[d - 1], bz_s.at[d - 1], bz_r.at[d - 1], zfrom(d) * NY + y, e)

    def pass_on(d):
        by_copy(d).wait()
        bzsend[d - 1] = (acc[d] + byrecv[d].astype(F32)).astype(BF16)
        bz_copy(d).start()

    def expert_pair(i, carry):
        d = jnp.where(i < 2, 0, jnp.where(i < 4, 1, 2 + lax.rem(i, 2)))
        other = jnp.logical_or(i == 1, jnp.logical_and(i >= 3, i < 6))
        p = jnp.where(other, oy, y) * NZ + zfrom(d)

        @pl.when(i == 1)
        def _():
            weights(9, 10)
            forward(1)

        @pl.when(jnp.logical_and(i >= 1, i < NZ))
        def _():
            az_copy(NG - 1, i).wait_recv()
            ay_copy(NG - 1, i).start()

        @pl.when(i == NT - 1)
        def _():
            pass_on(1)

        @pl.when(other)
        def _():
            for n in range(1, NG):
                ay_copy(n, d).wait_recv()

        x = jnp.concatenate([xs[n, p] for n in range(NG)], axis=0)
        h0 = jnp.dot(x, win[2 * p], preferred_element_type=F32)
        h1 = jnp.dot(x, win[2 * p + 1], preferred_element_type=F32)
        hid = gelu(jnp.where(upper, h0, h1))
        zero = jnp.zeros_like(hid)
        u0 = jnp.where(upper, hid, zero).astype(BF16)
        u1 = jnp.where(upper, zero, hid).astype(BF16)
        out = (jnp.dot(u0, wout[2 * p], preferred_element_type=F32)
               + jnp.dot(u1, wout[2 * p + 1], preferred_element_type=F32))

        @pl.when(other)
        def _():
            bsend[d] = out.astype(BF16)
            by_copy(d).start()

        @pl.when(jnp.logical_not(other))
        def _():
            acc[d] = out

        return carry

    lax.fori_loop(0, NT, expert_pair, 0)

    weights(10, 11)
    pass_on(2)
    weights(11, 12)
    pass_on(3)
    by_copy(0).wait()
    acc[0] += byrecv[0].astype(F32)
    for n in range(NG):
        for d in range(1, NZ):
            az_copy(n, d).wait_send()
        for d in range(NZ):
            ay_copy(n, d).wait_send()

    def c_copy(n):
        return remote(fin.at[cross_e[n]], g.at[g_at, me], c_s.at[n], c_r.at[n], t, cross_e[n])

    def block(at, h):
        return g.at[pl.ds(2 * h, 2), y * NZ + at]

    def gz_copy(d, h):
        return remote(block(z, h), block(z, h), s_s.at[h, NZ - 1 + d], s_r.at[h, NZ - 1 + d], zpeer(d) * NY + y, e)

    def cross(d, h):
        return remote(block(zfrom(d), h), block(zfrom(d), h), s_s.at[h, d], s_r.at[h, d], y_tok, e)

    def launch(h):
        cross(0, h).start()
        for d in range(1, NZ):
            gz_copy(d, h).start()

    @pl.when(core == 0)
    def _():
        c_copy(1).wait_recv()
        c_copy(2).wait_recv()
        launch(1)

    for d in range(1, NZ):
        bz_copy(d).wait()
    done = (acc[0] + bzrecv[0].astype(F32) + bzrecv[1].astype(F32) + bzrecv[2].astype(F32)).astype(BF16)
    for k in range(NE):
        fin[k] = done[:, k * feat:(k + 1) * feat]
    for n in range(NE - 1):
        c_copy(n).start()
    g[g_at, me] = fin[e]
    c_copy(0).wait_recv()

    @pl.when(core == 0)
    def _():
        launch(0)

    @pl.when(core == 1)
    def _():
        launch(1)
        c_copy(1).wait_recv()
        c_copy(2).wait_recv()
        launch(0)

    for h in (1, 0):
        for d in range(1, NZ):
            gz_copy(d, h).wait_recv()
            cross(d, h).start()
    for n in range(NE - 1):
        c_copy(n).wait_send()
    for i in range(NG):
        cw_copy(i).wait()
        cw_send(i).wait()
    outs = []
    for h in (1, 0):
        for d in range(NZ):
            cross(d, h).wait()
        at = pl.ds(2 * h, 2)
        outs.append(pltpu.make_async_copy(g.at[at], g_hbm.at[at], gsem.at[h]))
        outs[-1].start()
    for h in range(2):
        for d in range(1, NZ):
            gz_copy(d, h).wait_send()
    for out in outs:
        out.wait()


def combine_kernel(cw_hbm, g_ref, o_hbm, cw, vals, o, csem, osem):
    seqs, length, slots = cw.shape
    blocks, _, feat = g_ref.shape
    size = seqs // NG
    span = g_ref.shape[1] // NG

    def cw_in(i):
        return pltpu.make_async_copy(cw_hbm.at[pl.ds(i * size, size)], cw.at[pl.ds(i * size, size)], csem.at[i])

    def out(i):
        return pltpu.make_async_copy(o.at[pl.ds(i * size, size)], o_hbm.at[pl.ds(i * size, size)], osem.at[i])

    for i in range(NG):
        cw_in(i).start()
    row = lax.broadcasted_iota(jnp.int32, (blocks * span, blocks * span), 0)
    col = lax.broadcasted_iota(jnp.int32, (blocks * span, blocks * span), 1)
    slot = lax.rem(row, slots)
    per = slots // NE
    e = slot // per
    at = (2 * lax.rem(e, 2) + e // 2) * per + lax.rem(slot, per)
    order = jnp.where(col == at * size + row // slots, 1.0, 0.0).astype(BF16)
    for i in range(NG):
        part = g_ref[:, i * span:(i + 1) * span, :].reshape(blocks * span, feat)
        vals[i] = jnp.dot(order, part, preferred_element_type=F32).astype(BF16)
    for i in range(NG):
        cw_in(i).wait()
        for q in range(size):
            s = i * size + q
            o[s] = jnp.dot(cw[s], vals[i, q * slots:(q + 1) * slots], preferred_element_type=F32).astype(BF16)
        out(i).start()
    for i in range(NG):
        out(i).wait()


def fused(tokens, slot_params, w_in, w_out):
    seqs, length, width = tokens.shape
    own_w = slot_params.shape[1]
    slots = own_w * NE
    experts, _, ff = w_in.shape
    rows = seqs * own_w
    pair_rows = rows // NT
    own_rows = rows // NG
    span = own_rows // NT
    feat = width // NE
    tiles = width // LANES
    dma = pltpu.SemaphoreType.DMA
    any_spec = pl.BlockSpec(memory_space=pl.ANY)
    cw, g = pl.pallas_call(
        main_kernel,
        out_shape=(jax.ShapeDtypeStruct((seqs, length, slots), BF16),
                   jax.ShapeDtypeStruct((NE, NT, pair_rows, feat), BF16)),
        in_specs=[any_spec, pl.BlockSpec(memory_space=pltpu.VMEM), any_spec, any_spec],
        out_specs=(any_spec, any_spec),
        scratch_shapes=[
            pltpu.VMEM((TB, length, width), BF16),
            pltpu.VMEM((slots, width), BF16),
            pltpu.VMEM((width, slots), BF16),
            pltpu.VMEM((experts, width, ff), BF16),
            pltpu.VMEM((experts, ff, width), BF16),
            pltpu.VMEM((seqs, length // 2, slots), BF16),
            pltpu.VMEM((NG, tiles, own_rows, LANES), F32),
            pltpu.VMEM((NG, NZ, span, width), BF16),
            pltpu.VMEM((NG, NT, 8, LANES), F32),
            pltpu.VMEM((2, own_rows, LANES), F32),
            pltpu.VMEM((NG, NZ, span, width), BF16),
            pltpu.VMEM((NG, NZ, span, width), BF16),
            pltpu.VMEM((NG, NZ - 1, span, width), BF16),
            pltpu.VMEM((NG, span, width), F32),
            pltpu.VMEM((NG, NT, span, width), BF16),
            pltpu.VMEM((NZ, pair_rows, width), F32),
            pltpu.VMEM((NZ, pair_rows, width), BF16),
            pltpu.VMEM((NZ, pair_rows, width), BF16),
            pltpu.VMEM((NZ - 1, pair_rows, width), BF16),
            pltpu.VMEM((NZ - 1, pair_rows, width), BF16),
            pltpu.VMEM((NE, pair_rows, feat), BF16),
            pltpu.VMEM((NE, NT, pair_rows, feat), BF16),
            dma((TB,)), dma((2 * NT,)), dma((NG,)), dma((2,)),
            dma((NE - 1,)), dma((NE - 1,)),
            dma((NG,)), dma((NG,)),
            dma((NG, NT - 1)), dma((NG, NT - 1)),
            dma((NG,)), dma((NG,)),
            dma((NG, NZ - 1)), dma((NG, NZ - 1)),
            dma((NG, NZ - 1)), dma((NG, NZ - 1)),
            dma((NG, NZ)), dma((NG, NZ)),
            dma((NZ,)), dma((NZ,)),
            dma((NZ - 1,)), dma((NZ - 1,)),
            dma((NE - 1,)), dma((NE - 1,)),
        ],
        compiler_params=pltpu.CompilerParams(collective_id=0, has_side_effects=True, vmem_limit_bytes=60 << 20),
        name="dispatch_experts",
    )(tokens, slot_params.T, w_in, w_out)
    return pl.pallas_call(
        combine_kernel,
        out_shape=jax.ShapeDtypeStruct((seqs, length, feat), BF16),
        in_specs=[any_spec, pl.BlockSpec(memory_space=pltpu.VMEM)],
        out_specs=any_spec,
        scratch_shapes=[
            pltpu.VMEM((seqs, length, slots), BF16),
            pltpu.VMEM((NG, NE * NT * span, feat), BF16),
            pltpu.VMEM((seqs, length, feat), BF16),
            dma((NG,)), dma((NG,)),
        ],
        compiler_params=pltpu.CompilerParams(vmem_limit_bytes=60 << 20),
        name="combine",
    )(cw, g.reshape(NE * NT, pair_rows, feat))


def shards(tokens, slot_params, w_in, w_out):
    own_width = slot_params.shape[1]
    own_logits = jnp.einsum("std,dj->sjt", tokens, slot_params, preferred_element_type=jnp.float32)
    all_logits = lax.all_gather(own_logits, "exp", axis=1, tiled=True)
    local_max = jnp.max(own_logits, axis=2)
    slot_peak = lax.pmax(local_max, "tok")
    dexp = jnp.exp(own_logits - slot_peak[:, :, None])
    local_den = jnp.sum(dexp, axis=2)
    dweight = dexp.astype(jnp.bfloat16)
    local_sum = jnp.einsum("sjt,std->sjd", dweight, tokens, preferred_element_type=jnp.float32)
    slot_sum, slot_den = lax.psum((local_sum, local_den), "tok")
    slot_in = (slot_sum / slot_den[:, :, None]).astype(jnp.bfloat16)
    seq_count = tokens.shape[0]
    local_experts = w_in.shape[0]
    width = tokens.shape[2]
    grouped = slot_in.reshape(seq_count, local_experts, SLOTS_PER, width)
    hidden = jax.nn.gelu(
        jnp.einsum("sepd,edf->sepf", grouped, w_in, preferred_element_type=jnp.float32),
        approximate=True,
    ).astype(jnp.bfloat16)
    partial_out = jnp.einsum("sepf,efd->sepd", hidden, w_out, preferred_element_type=jnp.float32)
    partial_out = partial_out.reshape(seq_count, own_width, width)
    summed = lax.psum(partial_out, "tok").astype(jnp.bfloat16)
    slot_out = lax.all_to_all(summed, "exp", split_axis=2, concat_axis=1, tiled=True)
    comb_max = jnp.max(all_logits, axis=1)
    cexp = jnp.exp(all_logits - comb_max[:, None, :])
    cweight = (cexp / jnp.sum(cexp, axis=1)[:, None, :]).astype(jnp.bfloat16)
    mixed = jnp.einsum("sjt,sjd->std", cweight, slot_out, preferred_element_type=jnp.float32)
    return mixed.astype(jnp.bfloat16)


def solution(mesh):
    quick = mesh.shape["tok"] == NT and mesh.shape["exp"] == NE
    return jax.shard_map(
        fused if quick else shards,
        mesh=mesh,
        in_specs=(
            P(None, "tok", None),
            P(None, "exp"),
            P("exp", None, "tok"),
            P("exp", "tok", None),
        ),
        out_specs=P(None, "tok", "exp"),
        check_vma=False,
    )
```

```python
import functools

import jax
import jax.numpy as jnp
from jax import lax
from jax.experimental import pallas as pl
from jax.experimental.pallas import tpu as pltpu
from jax.sharding import PartitionSpec as P

SLOTS_PER = 2
NZ, NY = 4, 2
NT = NZ * NY
NE = 4
NG = 3
TB = 4
LANES = 128
MESH = pl.DeviceIdType.MESH
F32, BF16 = jnp.float32, jnp.bfloat16


def gelu(v):
    return 0.5 * v * (1.0 + jnp.tanh(0.7978845608 * (v + 0.044715 * (v * v * v))))


def main_kernel(
    tok_hbm, prm_ref, win_hbm, wout_hbm, cw_hbm, g_hbm,
    tbuf, prm, prm_t, win, wout, cwbuf, part, psend, st, wrow, yrecv, zsend, zrecv, facc, xs,
    acc, bsend, byrecv, bzsend, bzrecv, fin, g,
    tsem, wsem, cwsem, gsem,
    p_s, p_r, t_s, t_r, s_s, s_r, y_s, y_r, z_s, z_r, az_s, az_r, ay_s, ay_r,
    by_s, by_r, bz_s, bz_r, c_s, c_r,
):
    seqs, length, width = tok_hbm.shape
    half = length // 2
    own_w = prm_ref.shape[0]
    pair_rows = acc.shape[1]
    group = seqs // NG
    span = pair_rows // NG
    feat = g.shape[3]
    tiles = width // LANES
    packs = own_w // 8
    t = lax.axis_index("tok")
    e = lax.axis_index("exp")
    z, y = t // NY, t % NY
    oy = 1 - y
    me = y * NZ + z
    side, core = e // 2, lax.rem(e, 2)
    half_rows = pl.ds(pl.multiple_of(core * half, half), half)
    cross_e = (lax.rem(e + 2, NE), e + 1 - 2 * core, lax.rem(e + 2, NE) + 1 - 2 * core)
    g_at = 2 * core + side

    def remote(src, dst, ssem, rsem, tok, exp):
        return pltpu.make_async_remote_copy(
            src_ref=src, dst_ref=dst, send_sem=ssem, recv_sem=rsem,
            device_id={"tok": tok, "exp": exp}, device_id_type=MESH)

    def zpeer(d):
        return lax.rem(z + d, NZ)

    def zfrom(d):
        return lax.rem(z + NZ - d, NZ)

    def tok_copy(s):
        slot = lax.rem(s, TB)
        return pltpu.make_async_copy(tok_hbm.at[s], tbuf.at[slot], tsem.at[slot])

    def win_copy(p):
        return pltpu.make_async_copy(win_hbm.at[pl.ds(2 * p, 2)], win.at[pl.ds(2 * p, 2)], wsem.at[p])

    def wout_copy(p):
        return pltpu.make_async_copy(wout_hbm.at[pl.ds(2 * p, 2)], wout.at[pl.ds(2 * p, 2)], wsem.at[NT + p])

    def load_weights(n):
        @pl.when(n < NT)
        def _():
            win_copy(n).start()

        @pl.when(n >= NT)
        def _():
            wout_copy(n - NT).start()

    def cw_copy(i):
        at = pl.ds(i * group, group)
        return pltpu.make_async_copy(cwbuf.at[at], cw_hbm.at[at, half_rows], cwsem.at[i])

    def cw_send(i):
        at = pl.ds(i * group, group)
        return remote(cwbuf.at[at], cw_hbm.at[at, half_rows], t_s.at[i], t_r.at[i], t, e + 1 - 2 * core)

    def half_copy(n):
        slot = lax.rem(n, TB)
        return pltpu.make_async_copy(tok_hbm.at[n, half_rows], tbuf.at[slot, pl.ds(0, half)], tsem.at[slot])

    for s in range(TB - 1):
        tok_copy(s).start()

    barrier = pltpu.get_barrier_semaphore()
    for d in range(1, NT):
        pl.semaphore_signal(barrier, inc=1, device_id={"tok": lax.rem(t + d, NT), "exp": e}, device_id_type=MESH)
    for d in range(1, NE):
        pl.semaphore_signal(barrier, inc=1, device_id={"tok": t, "exp": lax.rem(e + d, NE)}, device_id_type=MESH)

    for i in range(NG):
        st[i, me] = jnp.ones((8, LANES), F32)
    lane = lax.broadcasted_iota(jnp.int32, (8, LANES), 1)

    def own_logits(s):
        return lax.dot_general(prm_ref[...], tbuf[lax.rem(s, TB)], (((1,), (1,)), ((), ())), preferred_element_type=F32)

    def emit(s, own):
        gi, in_group = s // group, lax.rem(s, group)
        peak = jnp.max(own, axis=1, keepdims=True)
        dx = jnp.exp(own - peak)
        den = jnp.sum(dx, axis=1, keepdims=True)
        ssum = jnp.dot(dx.astype(BF16), tbuf[lax.rem(s, TB)], preferred_element_type=F32)
        scaled = ssum / den
        for k in range(tiles):
            part[gi, k, pl.ds(in_group, own_w, stride=group), :] = scaled[:, k * LANES:(k + 1) * LANES]
        stats = st[gi, me]
        for a in range(packs):
            at = a * group + in_group
            stats = jnp.where(lane == at, peak[8 * a:8 * a + 8], jnp.where(lane == at + 64, den[8 * a:8 * a + 8], stats))
        st[gi, me] = stats

    def dispatch(s, own):
        @pl.when(s + TB - 1 < seqs)
        def _():
            tok_copy(s + TB - 1).start()

        @pl.when(s + TB - 1 >= seqs)
        def _():
            half_copy(s + TB - 1 - seqs).start()

        @pl.when(jnp.logical_and(s < NT, lax.rem(s, 2) == 1))
        def _():
            win_copy(s // 2).start()

        @pl.when(s >= NT)
        def _():
            win_copy(s - group).start()

        tok_copy(s + 1).wait()
        later = own_logits(s + 1)
        emit(s, own)
        return later

    y_tok = z * NY + oy

    def st_copy(i, d):
        return remote(st.at[i, me], st.at[i, me], s_s.at[i, d - 1], s_r.at[i, d - 1], lax.rem(t + d, NT), e)

    def y_copy(i):
        return remote(psend.at[i], yrecv.at[i], y_s.at[i], y_r.at[i], y_tok, e)

    def z_copy(i, d):
        zz = zpeer(d)
        return remote(zsend.at[i, zz], zrecv.at[i, d - 1], z_s.at[i, d - 1], z_r.at[i, d - 1], zz * NY + y, e)

    def az_copy(i, d):
        return remote(xs.at[i, me], xs.at[i, me], az_s.at[i, d - 1], az_r.at[i, d - 1], zpeer(d) * NY + y, e)

    def ay_copy(i, d):
        got = y * NZ + zfrom(d)
        return remote(xs.at[i, got], xs.at[i, got], ay_s.at[i, d], ay_r.at[i, d], y_tok, e)

    def pair_slice(p):
        return pl.ds(pl.multiple_of(p * span, span), span)

    def send_partial(i):
        for d in range(1, NT):
            st_copy(i, d).start()
        for zz in range(NZ):
            rows = pair_slice(oy * NZ + zz)
            for k in range(tiles):
                psend[i, zz, :, k * LANES:(k + 1) * LANES] = part[i, k, rows, :].astype(BF16)
        y_copy(i).start()

    def reduce_y(i):
        for d in range(1, NT):
            st_copy(i, d).wait()
        peaks = [st[i, r] for r in range(NT)]
        top = functools.reduce(jnp.maximum, peaks)
        total = jnp.zeros_like(top)
        for r in range(NT):
            total += pltpu.roll(peaks[r], 64, 1) * jnp.exp(peaks[r] - top)
        for n, r in enumerate((me, oy * NZ + z)):
            mine = st[i, r]
            w = pltpu.roll(mine, 64, 1) * jnp.exp(mine - top) / total
            for a in range(packs):
                for q in range(group):
                    at = a * group + q
                    wrow[n, pl.ds(8 * a * group + q, 8, stride=group), :] = jnp.broadcast_to(w[:, at:at + 1], (8, LANES))
        y_copy(i).wait()
        for d in (1, 2, 3, 0):
            zz = zpeer(d)
            rows = pair_slice(y * NZ + zz)
            w0, w1 = wrow[0, rows, :], wrow[1, rows, :]
            for k in range(tiles):
                cols = slice(k * LANES, (k + 1) * LANES)
                both = part[i, k, rows, :] * w0 + yrecv[i, zz, :, cols].astype(F32) * w1
                if d:
                    zsend[i, zz, :, cols] = both.astype(BF16)
                else:
                    facc[i, :, cols] = both
            if d:
                z_copy(i, d).start()

    def finish_z(i):
        for d in range(1, NZ):
            z_copy(i, d).wait()
        xs[i, me] = (facc[i] + zrecv[i, 0].astype(F32) + zrecv[i, 1].astype(F32) + zrecv[i, 2].astype(F32)).astype(BF16)
        ay_copy(i, 0).start()
        for d in range(1, NZ):
            az_copy(i, d).start()

    def forward(i):
        for d in range(1, NZ):
            az_copy(i, d).wait_recv()
            ay_copy(i, d).start()

    own_rows = pl.ds(pl.multiple_of(e * own_w, own_w), own_w)

    def p_copy(n):
        return remote(prm_ref, prm.at[own_rows], p_s.at[n], p_r.at[n], t, cross_e[n])

    def weigh(c, carry):
        early = seqs - 1 - group

        @pl.when(c + TB - 1 < seqs)
        def _():
            half_copy(c + TB - 1).start()

        @pl.when(2 * c < 2 * NT - early)
        def _():
            load_weights(2 * c + early)

            @pl.when(2 * c + 1 < 2 * NT - early)
            def _():
                load_weights(2 * c + 1 + early)

        half_copy(c).wait()
        logits = jnp.dot(tbuf[lax.rem(c, TB), 0:half, :], prm_t[...], preferred_element_type=F32)
        ex = jnp.exp(logits - jnp.max(logits, axis=1, keepdims=True))
        cwbuf[c] = (ex / jnp.sum(ex, axis=1, keepdims=True)).astype(BF16)

        @pl.when(lax.rem(c, group) == group - 1)
        def _():
            cw_copy(c // group).start()
            cw_send(c // group).start()

        return carry

    def weights(a, b):
        lax.fori_loop(a, b, weigh, 0)

    def run(a, b, logits):
        return lax.fori_loop(a, b, dispatch, logits)

    tok_copy(0).wait()
    own = own_logits(0)
    own = run(0, 4, own)
    pl.semaphore_wait(barrier, NT + NE - 2)
    send_partial(0)
    for n in range(NE - 1):
        p_copy(n).start()
    prm[own_rows, :] = prm_ref[...]
    own = run(4, 8, own)
    send_partial(1)
    reduce_y(0)
    own = run(8, 11, own)
    emit(seqs - 1, own)
    send_partial(2)
    half_copy(2).start()
    reduce_y(1)
    for n in range(NE - 1):
        p_copy(n).wait()
    prm_t[...] = prm[...].astype(F32).T.astype(BF16)
    weights(0, 2)
    finish_z(0)
    weights(2, 4)
    reduce_y(2)
    finish_z(1)
    weights(4, 6)
    forward(0)
    weights(6, 9)
    finish_z(2)
    weights(9, 10)
    for p in range(NT):
        win_copy(p).wait()
    for p in range(NT):
        wout_copy(p).wait()
    ay_copy(0, 0).wait_recv()
    for d in range(1, NZ):
        ay_copy(0, d).wait_recv()

    upper = lax.rem(lax.broadcasted_iota(jnp.int32, (pair_rows, 1), 0), span) < span // 2

    def by_copy(d):
        return remote(bsend.at[d], byrecv.at[d], by_s.at[d], by_r.at[d], y_tok, e)

    def bz_copy(d):
        return remote(bzsend.at[d - 1], bzrecv.at[d - 1], bz_s.at[d - 1], bz_r.at[d - 1], zfrom(d) * NY + y, e)

    def pass_on(d):
        by_copy(d).wait()
        bzsend[d - 1] = (acc[d] + byrecv[d].astype(F32)).astype(BF16)
        bz_copy(d).start()

    def expert_pair(i, carry):
        d = i // 2
        other = lax.rem(i, 2) == 1
        p = jnp.where(other, oy, y) * NZ + zfrom(d)

        @pl.when(i == 1)
        def _():
            forward(1)

        @pl.when(jnp.logical_and(i >= 1, i < NZ))
        def _():
            az_copy(NG - 1, i).wait_recv()
            ay_copy(NG - 1, i).start()

        @pl.when(i == NT - 1)
        def _():
            pass_on(1)

        @pl.when(other)
        def _():
            for n in range(1, NG):
                ay_copy(n, d).wait_recv()

        x = jnp.concatenate([xs[n, p] for n in range(NG)], axis=0)
        h0 = jnp.dot(x, win[2 * p], preferred_element_type=F32)
        h1 = jnp.dot(x, win[2 * p + 1], preferred_element_type=F32)
        hid = gelu(jnp.where(upper, h0, h1))
        zero = jnp.zeros_like(hid)
        u0 = jnp.where(upper, hid, zero).astype(BF16)
        u1 = jnp.where(upper, zero, hid).astype(BF16)
        out = (jnp.dot(u0, wout[2 * p], preferred_element_type=F32)
               + jnp.dot(u1, wout[2 * p + 1], preferred_element_type=F32))

        @pl.when(other)
        def _():
            bsend[d] = out.astype(BF16)
            by_copy(d).start()

        @pl.when(jnp.logical_not(other))
        def _():
            acc[d] = out

        return carry

    lax.fori_loop(0, NT, expert_pair, 0)

    weights(10, 11)
    pass_on(2)
    weights(11, 12)
    pass_on(3)
    by_copy(0).wait()
    acc[0] += byrecv[0].astype(F32)
    for n in range(NG):
        for d in range(1, NZ):
            az_copy(n, d).wait_send()
        for d in range(NZ):
            ay_copy(n, d).wait_send()

    def c_copy(n):
        return remote(fin.at[cross_e[n]], g.at[g_at, me], c_s.at[n], c_r.at[n], t, cross_e[n])

    def block(at, h):
        return g.at[pl.ds(2 * h, 2), y * NZ + at]

    def gz_copy(d, h):
        return remote(block(z, h), block(z, h), s_s.at[h, NZ - 1 + d], s_r.at[h, NZ - 1 + d], zpeer(d) * NY + y, e)

    def cross(d, h):
        return remote(block(zfrom(d), h), block(zfrom(d), h), s_s.at[h, d], s_r.at[h, d], y_tok, e)

    def launch(h):
        cross(0, h).start()
        for d in range(1, NZ):
            gz_copy(d, h).start()

    @pl.when(core == 0)
    def _():
        c_copy(1).wait_recv()
        c_copy(2).wait_recv()
        launch(1)

    for d in range(1, NZ):
        bz_copy(d).wait()
    done = (acc[0] + bzrecv[0].astype(F32) + bzrecv[1].astype(F32) + bzrecv[2].astype(F32)).astype(BF16)
    for k in range(NE):
        fin[k] = done[:, k * feat:(k + 1) * feat]
    for n in range(NE - 1):
        c_copy(n).start()
    g[g_at, me] = fin[e]
    c_copy(0).wait_recv()

    @pl.when(core == 0)
    def _():
        launch(0)

    @pl.when(core == 1)
    def _():
        launch(1)
        c_copy(1).wait_recv()
        c_copy(2).wait_recv()
        launch(0)

    for h in (1, 0):
        for d in range(1, NZ):
            gz_copy(d, h).wait_recv()
            cross(d, h).start()
    for n in range(NE - 1):
        c_copy(n).wait_send()
    for i in range(NG):
        cw_copy(i).wait()
        cw_send(i).wait()
    outs = []
    for h in (1, 0):
        for d in range(NZ):
            cross(d, h).wait()
        at = pl.ds(2 * h, 2)
        outs.append(pltpu.make_async_copy(g.at[at], g_hbm.at[at], gsem.at[h]))
        outs[-1].start()
    for h in range(2):
        for d in range(1, NZ):
            gz_copy(d, h).wait_send()
    for out in outs:
        out.wait()


def combine_kernel(cw_hbm, g_ref, o_hbm, cw, vals, o, csem, osem):
    seqs, length, slots = cw.shape
    blocks, _, feat = g_ref.shape
    size = seqs // NG
    span = g_ref.shape[1] // NG

    def cw_in(i):
        return pltpu.make_async_copy(cw_hbm.at[pl.ds(i * size, size)], cw.at[pl.ds(i * size, size)], csem.at[i])

    def out(i):
        return pltpu.make_async_copy(o.at[pl.ds(2 * i, 2)], o_hbm.at[pl.ds(2 * i, 2)], osem.at[i])

    for i in range(NG):
        cw_in(i).start()
    row = lax.broadcasted_iota(jnp.int32, (blocks * span, blocks * span), 0)
    col = lax.broadcasted_iota(jnp.int32, (blocks * span, blocks * span), 1)
    slot = lax.rem(row, slots)
    per = slots // NE
    e = slot // per
    at = (2 * lax.rem(e, 2) + e // 2) * per + lax.rem(slot, per)
    order = jnp.where(col == at * size + row // slots, 1.0, 0.0).astype(BF16)
    for i in range(NG):
        part = g_ref[:, i * span:(i + 1) * span, :].reshape(blocks * span, feat)
        vals[i] = jnp.dot(order, part, preferred_element_type=F32).astype(BF16)
    for i in range(NG):
        cw_in(i).wait()
        for q in range(size):
            s = i * size + q
            o[s] = jnp.dot(cw[s], vals[i, q * slots:(q + 1) * slots], preferred_element_type=F32).astype(BF16)
            if q % 2:
                out(s // 2).start()
    for i in range(seqs // 2):
        out(i).wait()


def fused(tokens, slot_params, w_in, w_out):
    seqs, length, width = tokens.shape
    own_w = slot_params.shape[1]
    slots = own_w * NE
    experts, _, ff = w_in.shape
    rows = seqs * own_w
    pair_rows = rows // NT
    own_rows = rows // NG
    span = own_rows // NT
    feat = width // NE
    tiles = width // LANES
    dma = pltpu.SemaphoreType.DMA
    any_spec = pl.BlockSpec(memory_space=pl.ANY)
    cw, g = pl.pallas_call(
        main_kernel,
        out_shape=(jax.ShapeDtypeStruct((seqs, length, slots), BF16),
                   jax.ShapeDtypeStruct((NE, NT, pair_rows, feat), BF16)),
        in_specs=[any_spec, pl.BlockSpec(memory_space=pltpu.VMEM), any_spec, any_spec],
        out_specs=(any_spec, any_spec),
        scratch_shapes=[
            pltpu.VMEM((TB, length, width), BF16),
            pltpu.VMEM((slots, width), BF16),
            pltpu.VMEM((width, slots), BF16),
            pltpu.VMEM((experts, width, ff), BF16),
            pltpu.VMEM((experts, ff, width), BF16),
            pltpu.VMEM((seqs, length // 2, slots), BF16),
            pltpu.VMEM((NG, tiles, own_rows, LANES), F32),
            pltpu.VMEM((NG, NZ, span, width), BF16),
            pltpu.VMEM((NG, NT, 8, LANES), F32),
            pltpu.VMEM((2, own_rows, LANES), F32),
            pltpu.VMEM((NG, NZ, span, width), BF16),
            pltpu.VMEM((NG, NZ, span, width), BF16),
            pltpu.VMEM((NG, NZ - 1, span, width), BF16),
            pltpu.VMEM((NG, span, width), F32),
            pltpu.VMEM((NG, NT, span, width), BF16),
            pltpu.VMEM((NZ, pair_rows, width), F32),
            pltpu.VMEM((NZ, pair_rows, width), BF16),
            pltpu.VMEM((NZ, pair_rows, width), BF16),
            pltpu.VMEM((NZ - 1, pair_rows, width), BF16),
            pltpu.VMEM((NZ - 1, pair_rows, width), BF16),
            pltpu.VMEM((NE, pair_rows, feat), BF16),
            pltpu.VMEM((NE, NT, pair_rows, feat), BF16),
            dma((TB,)), dma((2 * NT,)), dma((NG,)), dma((2,)),
            dma((NE - 1,)), dma((NE - 1,)),
            dma((NG,)), dma((NG,)),
            dma((NG, NT - 1)), dma((NG, NT - 1)),
            dma((NG,)), dma((NG,)),
            dma((NG, NZ - 1)), dma((NG, NZ - 1)),
            dma((NG, NZ - 1)), dma((NG, NZ - 1)),
            dma((NG, NZ)), dma((NG, NZ)),
            dma((NZ,)), dma((NZ,)),
            dma((NZ - 1,)), dma((NZ - 1,)),
            dma((NE - 1,)), dma((NE - 1,)),
        ],
        compiler_params=pltpu.CompilerParams(collective_id=0, has_side_effects=True, vmem_limit_bytes=60 << 20),
        name="dispatch_experts",
    )(tokens, slot_params.T, w_in, w_out)
    return pl.pallas_call(
        combine_kernel,
        out_shape=jax.ShapeDtypeStruct((seqs, length, feat), BF16),
        in_specs=[any_spec, pl.BlockSpec(memory_space=pltpu.VMEM)],
        out_specs=any_spec,
        scratch_shapes=[
            pltpu.VMEM((seqs, length, slots), BF16),
            pltpu.VMEM((NG, NE * NT * span, feat), BF16),
            pltpu.VMEM((seqs, length, feat), BF16),
            dma((NG,)), dma((seqs // 2,)),
        ],
        compiler_params=pltpu.CompilerParams(vmem_limit_bytes=60 << 20),
        name="combine",
    )(cw, g.reshape(NE * NT, pair_rows, feat))


def shards(tokens, slot_params, w_in, w_out):
    own_width = slot_params.shape[1]
    own_logits = jnp.einsum("std,dj->sjt", tokens, slot_params, preferred_element_type=jnp.float32)
    all_logits = lax.all_gather(own_logits, "exp", axis=1, tiled=True)
    local_max = jnp.max(own_logits, axis=2)
    slot_peak = lax.pmax(local_max, "tok")
    dexp = jnp.exp(own_logits - slot_peak[:, :, None])
    local_den = jnp.sum(dexp, axis=2)
    dweight = dexp.astype(jnp.bfloat16)
    local_sum = jnp.einsum("sjt,std->sjd", dweight, tokens, preferred_element_type=jnp.float32)
    slot_sum, slot_den = lax.psum((local_sum, local_den), "tok")
    slot_in = (slot_sum / slot_den[:, :, None]).astype(jnp.bfloat16)
    seq_count = tokens.shape[0]
    local_experts = w_in.shape[0]
    width = tokens.shape[2]
    grouped = slot_in.reshape(seq_count, local_experts, SLOTS_PER, width)
    hidden = jax.nn.gelu(
        jnp.einsum("sepd,edf->sepf", grouped, w_in, preferred_element_type=jnp.float32),
        approximate=True,
    ).astype(jnp.bfloat16)
    partial_out = jnp.einsum("sepf,efd->sepd", hidden, w_out, preferred_element_type=jnp.float32)
    partial_out = partial_out.reshape(seq_count, own_width, width)
    summed = lax.psum(partial_out, "tok").astype(jnp.bfloat16)
    slot_out = lax.all_to_all(summed, "exp", split_axis=2, concat_axis=1, tiled=True)
    comb_max = jnp.max(all_logits, axis=1)
    cexp = jnp.exp(all_logits - comb_max[:, None, :])
    cweight = (cexp / jnp.sum(cexp, axis=1)[:, None, :]).astype(jnp.bfloat16)
    mixed = jnp.einsum("sjt,sjd->std", cweight, slot_out, preferred_element_type=jnp.float32)
    return mixed.astype(jnp.bfloat16)


def solution(mesh):
    quick = mesh.shape["tok"] == NT and mesh.shape["exp"] == NE
    return jax.shard_map(
        fused if quick else shards,
        mesh=mesh,
        in_specs=(
            P(None, "tok", None),
            P(None, "exp"),
            P("exp", None, "tok"),
            P("exp", "tok", None),
        ),
        out_specs=P(None, "tok", "exp"),
        check_vma=False,
    )
```

```python
import functools

import jax
import jax.numpy as jnp
from jax import lax
from jax.experimental import pallas as pl
from jax.experimental.pallas import tpu as pltpu
from jax.sharding import PartitionSpec as P

SLOTS_PER = 2
NZ, NY = 4, 2
NT = NZ * NY
NE = 4
NG = 3
TB = 4
LANES = 128
MESH = pl.DeviceIdType.MESH
F32, BF16 = jnp.float32, jnp.bfloat16


def gelu(v):
    return 0.5 * v * (1.0 + jnp.tanh(0.7978845608 * (v + 0.044715 * (v * v * v))))


def main_kernel(
    tok_hbm, prm_ref, win_hbm, wout_hbm, cw_hbm, g_hbm,
    tbuf, prm, prm_t, win, wout, cwbuf, part, psend, st, wrow, yrecv, zsend, zrecv, facc, xs,
    acc, bsend, byrecv, bzsend, bzrecv, fin, g,
    tsem, wsem, cwsem, gsem,
    p_s, p_r, t_s, t_r, s_s, s_r, y_s, y_r, z_s, z_r, az_s, az_r, ay_s, ay_r,
    by_s, by_r, bz_s, bz_r, c_s, c_r,
):
    seqs, length, width = tok_hbm.shape
    half = length // 2
    own_w = prm_ref.shape[0]
    pair_rows = acc.shape[1]
    group = seqs // NG
    span = pair_rows // NG
    feat = g.shape[3]
    tiles = width // LANES
    packs = own_w // 8
    t = lax.axis_index("tok")
    e = lax.axis_index("exp")
    z, y = t // NY, t % NY
    oy = 1 - y
    me = y * NZ + z
    side, core = e // 2, lax.rem(e, 2)
    half_rows = pl.ds(pl.multiple_of(core * half, half), half)
    cross_e = (lax.rem(e + 2, NE), e + 1 - 2 * core, lax.rem(e + 2, NE) + 1 - 2 * core)
    g_at = 2 * core + side

    def remote(src, dst, ssem, rsem, tok, exp):
        return pltpu.make_async_remote_copy(
            src_ref=src, dst_ref=dst, send_sem=ssem, recv_sem=rsem,
            device_id={"tok": tok, "exp": exp}, device_id_type=MESH)

    def zpeer(d):
        return lax.rem(z + d, NZ)

    def zfrom(d):
        return lax.rem(z + NZ - d, NZ)

    def tok_copy(s):
        slot = lax.rem(s, TB)
        return pltpu.make_async_copy(tok_hbm.at[s], tbuf.at[slot], tsem.at[slot])

    def win_copy(p):
        return pltpu.make_async_copy(win_hbm.at[pl.ds(2 * p, 2)], win.at[pl.ds(2 * p, 2)], wsem.at[p])

    def wout_copy(p):
        return pltpu.make_async_copy(wout_hbm.at[pl.ds(2 * p, 2)], wout.at[pl.ds(2 * p, 2)], wsem.at[NT + p])

    def load_weights(n):
        @pl.when(n < NT)
        def _():
            win_copy(n).start()

        @pl.when(n >= NT)
        def _():
            wout_copy(n - NT).start()

    def cw_copy(i):
        at = pl.ds(i * group, group)
        return pltpu.make_async_copy(cwbuf.at[at], cw_hbm.at[at, half_rows], cwsem.at[i])

    def cw_send(i):
        at = pl.ds(i * group, group)
        return remote(cwbuf.at[at], cw_hbm.at[at, half_rows], t_s.at[i], t_r.at[i], t, e + 1 - 2 * core)

    def half_copy(n):
        slot = lax.rem(n, TB)
        return pltpu.make_async_copy(tok_hbm.at[n, half_rows], tbuf.at[slot, pl.ds(0, half)], tsem.at[slot])

    for s in range(TB - 1):
        tok_copy(s).start()

    barrier = pltpu.get_barrier_semaphore()
    for d in range(1, NT):
        pl.semaphore_signal(barrier, inc=1, device_id={"tok": lax.rem(t + d, NT), "exp": e}, device_id_type=MESH)
    for d in range(1, NE):
        pl.semaphore_signal(barrier, inc=1, device_id={"tok": t, "exp": lax.rem(e + d, NE)}, device_id_type=MESH)

    for i in range(NG):
        st[i, me] = jnp.ones((8, LANES), F32)
    lane = lax.broadcasted_iota(jnp.int32, (8, LANES), 1)

    def own_logits(s):
        return lax.dot_general(prm_ref[...], tbuf[lax.rem(s, TB)], (((1,), (1,)), ((), ())), preferred_element_type=F32)

    def emit(s, own):
        gi, in_group = s // group, lax.rem(s, group)
        peak = jnp.max(own, axis=1, keepdims=True)
        dx = jnp.exp(own - peak)
        den = jnp.sum(dx, axis=1, keepdims=True)
        ssum = jnp.dot(dx.astype(BF16), tbuf[lax.rem(s, TB)], preferred_element_type=F32)
        scaled = ssum / den
        for k in range(tiles):
            part[gi, k, pl.ds(in_group, own_w, stride=group), :] = scaled[:, k * LANES:(k + 1) * LANES]
        stats = st[gi, me]
        for a in range(packs):
            at = a * group + in_group
            stats = jnp.where(lane == at, peak[8 * a:8 * a + 8], jnp.where(lane == at + 64, den[8 * a:8 * a + 8], stats))
        st[gi, me] = stats

    def dispatch(s, own):
        @pl.when(s + TB - 1 < seqs)
        def _():
            tok_copy(s + TB - 1).start()

        @pl.when(s + TB - 1 >= seqs)
        def _():
            half_copy(s + TB - 1 - seqs).start()

        @pl.when(jnp.logical_and(s < NT, lax.rem(s, 2) == 1))
        def _():
            win_copy(s // 2).start()

        @pl.when(s >= NT)
        def _():
            win_copy(s - group).start()

        tok_copy(s + 1).wait()
        later = own_logits(s + 1)
        emit(s, own)
        return later

    y_tok = z * NY + oy

    def st_copy(i, d):
        return remote(st.at[i, me], st.at[i, me], s_s.at[i, d - 1], s_r.at[i, d - 1], lax.rem(t + d, NT), e)

    def y_copy(i):
        return remote(psend.at[i], yrecv.at[i], y_s.at[i], y_r.at[i], y_tok, e)

    def z_copy(i, d):
        zz = zpeer(d)
        return remote(zsend.at[i, zz], zrecv.at[i, d - 1], z_s.at[i, d - 1], z_r.at[i, d - 1], zz * NY + y, e)

    def az_copy(i, d):
        return remote(xs.at[i, me], xs.at[i, me], az_s.at[i, d - 1], az_r.at[i, d - 1], zpeer(d) * NY + y, e)

    def ay_copy(i, d):
        got = y * NZ + zfrom(d)
        return remote(xs.at[i, got], xs.at[i, got], ay_s.at[i, d], ay_r.at[i, d], y_tok, e)

    def pair_slice(p):
        return pl.ds(pl.multiple_of(p * span, span), span)

    def send_partial(i):
        for d in range(1, NT):
            st_copy(i, d).start()
        for zz in range(NZ):
            rows = pair_slice(oy * NZ + zz)
            for k in range(tiles):
                psend[i, zz, :, k * LANES:(k + 1) * LANES] = part[i, k, rows, :].astype(BF16)
        y_copy(i).start()

    def reduce_y(i):
        for d in range(1, NT):
            st_copy(i, d).wait()
        peaks = [st[i, r] for r in range(NT)]
        top = functools.reduce(jnp.maximum, peaks)
        total = jnp.zeros_like(top)
        for r in range(NT):
            total += pltpu.roll(peaks[r], 64, 1) * jnp.exp(peaks[r] - top)
        for n, r in enumerate((me, oy * NZ + z)):
            mine = st[i, r]
            w = pltpu.roll(mine, 64, 1) * jnp.exp(mine - top) / total
            for a in range(packs):
                for q in range(group):
                    at = a * group + q
                    wrow[n, pl.ds(8 * a * group + q, 8, stride=group), :] = jnp.broadcast_to(w[:, at:at + 1], (8, LANES))
        y_copy(i).wait()
        for d in (1, 2, 3, 0):
            zz = zpeer(d)
            rows = pair_slice(y * NZ + zz)
            w0, w1 = wrow[0, rows, :], wrow[1, rows, :]
            for k in range(tiles):
                cols = slice(k * LANES, (k + 1) * LANES)
                both = part[i, k, rows, :] * w0 + yrecv[i, zz, :, cols].astype(F32) * w1
                if d:
                    zsend[i, zz, :, cols] = both.astype(BF16)
                else:
                    facc[i, :, cols] = both
            if d:
                z_copy(i, d).start()

    def finish_z(i):
        for d in range(1, NZ):
            z_copy(i, d).wait()
        xs[i, me] = (facc[i] + zrecv[i, 0].astype(F32) + zrecv[i, 1].astype(F32) + zrecv[i, 2].astype(F32)).astype(BF16)
        for d in range(1, NZ):
            az_copy(i, d).start()
        ay_copy(i, 0).start()

    def forward(i):
        for d in range(1, NZ):
            az_copy(i, d).wait_recv()
            ay_copy(i, d).start()

    own_rows = pl.ds(pl.multiple_of(e * own_w, own_w), own_w)

    def p_copy(n):
        return remote(prm_ref, prm.at[own_rows], p_s.at[n], p_r.at[n], t, cross_e[n])

    def weigh(c, carry):
        early = seqs - 1 - group

        @pl.when(c + TB - 1 < seqs)
        def _():
            half_copy(c + TB - 1).start()

        @pl.when(2 * c < 2 * NT - early)
        def _():
            load_weights(2 * c + early)

            @pl.when(2 * c + 1 < 2 * NT - early)
            def _():
                load_weights(2 * c + 1 + early)

        half_copy(c).wait()
        logits = jnp.dot(tbuf[lax.rem(c, TB), 0:half, :], prm_t[...], preferred_element_type=F32)
        ex = jnp.exp(logits - jnp.max(logits, axis=1, keepdims=True))
        cwbuf[c] = (ex / jnp.sum(ex, axis=1, keepdims=True)).astype(BF16)

        @pl.when(lax.rem(c, group) == group - 1)
        def _():
            cw_copy(c // group).start()
            cw_send(c // group).start()

        return carry

    def weights(a, b):
        lax.fori_loop(a, b, weigh, 0)

    def run(a, b, logits):
        return lax.fori_loop(a, b, dispatch, logits)

    tok_copy(0).wait()
    own = own_logits(0)
    own = run(0, 4, own)
    pl.semaphore_wait(barrier, NT + NE - 2)
    send_partial(0)
    for n in range(NE - 1):
        p_copy(n).start()
    prm[own_rows, :] = prm_ref[...]
    own = run(4, 8, own)
    send_partial(1)
    reduce_y(0)
    own = run(8, 11, own)
    emit(seqs - 1, own)
    send_partial(2)
    half_copy(2).start()
    reduce_y(1)
    for n in range(NE - 1):
        p_copy(n).wait()
    prm_t[...] = prm[...].astype(F32).T.astype(BF16)
    weights(0, 2)
    finish_z(0)
    weights(2, 4)
    reduce_y(2)
    finish_z(1)
    weights(4, 6)
    forward(0)
    weights(6, 9)
    finish_z(2)
    weights(9, 10)
    for p in range(NT):
        win_copy(p).wait()
    for p in range(NT):
        wout_copy(p).wait()
    ay_copy(0, 0).wait_recv()
    for d in range(1, NZ):
        ay_copy(0, d).wait_recv()

    upper = lax.rem(lax.broadcasted_iota(jnp.int32, (pair_rows, 1), 0), span) < span // 2

    def by_copy(d):
        return remote(bsend.at[d], byrecv.at[d], by_s.at[d], by_r.at[d], y_tok, e)

    def bz_copy(d):
        return remote(bzsend.at[d - 1], bzrecv.at[d - 1], bz_s.at[d - 1], bz_r.at[d - 1], zfrom(d) * NY + y, e)

    def pass_on(d):
        by_copy(d).wait()
        bzsend[d - 1] = (acc[d] + byrecv[d].astype(F32)).astype(BF16)
        bz_copy(d).start()

    def expert_pair(i, carry):
        d = i // 2
        other = lax.rem(i, 2) == 1
        p = jnp.where(other, oy, y) * NZ + zfrom(d)

        @pl.when(i == 1)
        def _():
            forward(1)

        @pl.when(jnp.logical_and(i >= 1, i < NZ))
        def _():
            az_copy(NG - 1, i).wait_recv()
            ay_copy(NG - 1, i).start()

        @pl.when(i == NT - 1)
        def _():
            pass_on(1)

        @pl.when(other)
        def _():
            for n in range(1, NG):
                ay_copy(n, d).wait_recv()

        x = jnp.concatenate([xs[n, p] for n in range(NG)], axis=0)
        h0 = jnp.dot(x, win[2 * p], preferred_element_type=F32)
        h1 = jnp.dot(x, win[2 * p + 1], preferred_element_type=F32)
        hid = gelu(jnp.where(upper, h0, h1))
        zero = jnp.zeros_like(hid)
        u0 = jnp.where(upper, hid, zero).astype(BF16)
        u1 = jnp.where(upper, zero, hid).astype(BF16)
        out = (jnp.dot(u0, wout[2 * p], preferred_element_type=F32)
               + jnp.dot(u1, wout[2 * p + 1], preferred_element_type=F32))

        @pl.when(other)
        def _():
            bsend[d] = out.astype(BF16)
            by_copy(d).start()

        @pl.when(jnp.logical_not(other))
        def _():
            acc[d] = out

        return carry

    lax.fori_loop(0, NT, expert_pair, 0)

    weights(10, 11)
    pass_on(2)
    weights(11, 12)
    pass_on(3)
    by_copy(0).wait()
    acc[0] += byrecv[0].astype(F32)
    for n in range(NG):
        for d in range(1, NZ):
            az_copy(n, d).wait_send()
        for d in range(NZ):
            ay_copy(n, d).wait_send()

    def c_copy(n):
        return remote(fin.at[cross_e[n]], g.at[g_at, me], c_s.at[n], c_r.at[n], t, cross_e[n])

    def block(at, h):
        return g.at[pl.ds(2 * h, 2), y * NZ + at]

    def gz_copy(d, h):
        return remote(block(z, h), block(z, h), s_s.at[h, NZ - 1 + d], s_r.at[h, NZ - 1 + d], zpeer(d) * NY + y, e)

    def cross(d, h):
        return remote(block(zfrom(d), h), block(zfrom(d), h), s_s.at[h, d], s_r.at[h, d], y_tok, e)

    def launch(h):
        for d in range(1, NZ):
            gz_copy(d, h).start()
        cross(0, h).start()

    @pl.when(core == 0)
    def _():
        c_copy(1).wait_recv()
        c_copy(2).wait_recv()
        launch(1)

    for d in range(1, NZ):
        bz_copy(d).wait()
    done = (acc[0] + bzrecv[0].astype(F32) + bzrecv[1].astype(F32) + bzrecv[2].astype(F32)).astype(BF16)
    for k in range(NE):
        fin[k] = done[:, k * feat:(k + 1) * feat]
    for n in range(NE - 1):
        c_copy(n).start()
    g[g_at, me] = fin[e]
    c_copy(0).wait_recv()

    @pl.when(core == 0)
    def _():
        launch(0)

    @pl.when(core == 1)
    def _():
        launch(1)
        c_copy(1).wait_recv()
        c_copy(2).wait_recv()
        launch(0)

    for h in (1, 0):
        for d in range(1, NZ):
            gz_copy(d, h).wait_recv()
            cross(d, h).start()
    for n in range(NE - 1):
        c_copy(n).wait_send()
    for i in range(NG):
        cw_copy(i).wait()
        cw_send(i).wait()
    outs = []
    for h in (1, 0):
        for d in range(NZ):
            cross(d, h).wait()
        at = pl.ds(2 * h, 2)
        outs.append(pltpu.make_async_copy(g.at[at], g_hbm.at[at], gsem.at[h]))
        outs[-1].start()
    for h in range(2):
        for d in range(1, NZ):
            gz_copy(d, h).wait_send()
    for out in outs:
        out.wait()


def combine_kernel(cw_hbm, g_ref, o_hbm, cw, vals, o, csem, osem):
    seqs, length, slots = cw.shape
    blocks, _, feat = g_ref.shape
    size = seqs // NG
    span = g_ref.shape[1] // NG

    def cw_in(i):
        return pltpu.make_async_copy(cw_hbm.at[pl.ds(i * size, size)], cw.at[pl.ds(i * size, size)], csem.at[i])

    def out(i):
        return pltpu.make_async_copy(o.at[pl.ds(2 * i, 2)], o_hbm.at[pl.ds(2 * i, 2)], osem.at[i])

    for i in range(NG):
        cw_in(i).start()
    row = lax.broadcasted_iota(jnp.int32, (blocks * span, blocks * span), 0)
    col = lax.broadcasted_iota(jnp.int32, (blocks * span, blocks * span), 1)
    slot = lax.rem(row, slots)
    per = slots // NE
    e = slot // per
    at = (2 * lax.rem(e, 2) + e // 2) * per + lax.rem(slot, per)
    order = jnp.where(col == at * size + row // slots, 1.0, 0.0).astype(BF16)
    for i in range(NG):
        part = g_ref[:, i * span:(i + 1) * span, :].reshape(blocks * span, feat)
        vals[i] = jnp.dot(order, part, preferred_element_type=F32).astype(BF16)
    for i in range(NG):
        cw_in(i).wait()
        for q in range(size):
            s = i * size + q
            o[s] = jnp.dot(cw[s], vals[i, q * slots:(q + 1) * slots], preferred_element_type=F32).astype(BF16)
            if q % 2:
                out(s // 2).start()
    for i in range(seqs // 2):
        out(i).wait()


def fused(tokens, slot_params, w_in, w_out):
    seqs, length, width = tokens.shape
    own_w = slot_params.shape[1]
    slots = own_w * NE
    experts, _, ff = w_in.shape
    rows = seqs * own_w
    pair_rows = rows // NT
    own_rows = rows // NG
    span = own_rows // NT
    feat = width // NE
    tiles = width // LANES
    dma = pltpu.SemaphoreType.DMA
    any_spec = pl.BlockSpec(memory_space=pl.ANY)
    cw, g = pl.pallas_call(
        main_kernel,
        out_shape=(jax.ShapeDtypeStruct((seqs, length, slots), BF16),
                   jax.ShapeDtypeStruct((NE, NT, pair_rows, feat), BF16)),
        in_specs=[any_spec, pl.BlockSpec(memory_space=pltpu.VMEM), any_spec, any_spec],
        out_specs=(any_spec, any_spec),
        scratch_shapes=[
            pltpu.VMEM((TB, length, width), BF16),
            pltpu.VMEM((slots, width), BF16),
            pltpu.VMEM((width, slots), BF16),
            pltpu.VMEM((experts, width, ff), BF16),
            pltpu.VMEM((experts, ff, width), BF16),
            pltpu.VMEM((seqs, length // 2, slots), BF16),
            pltpu.VMEM((NG, tiles, own_rows, LANES), F32),
            pltpu.VMEM((NG, NZ, span, width), BF16),
            pltpu.VMEM((NG, NT, 8, LANES), F32),
            pltpu.VMEM((2, own_rows, LANES), F32),
            pltpu.VMEM((NG, NZ, span, width), BF16),
            pltpu.VMEM((NG, NZ, span, width), BF16),
            pltpu.VMEM((NG, NZ - 1, span, width), BF16),
            pltpu.VMEM((NG, span, width), F32),
            pltpu.VMEM((NG, NT, span, width), BF16),
            pltpu.VMEM((NZ, pair_rows, width), F32),
            pltpu.VMEM((NZ, pair_rows, width), BF16),
            pltpu.VMEM((NZ, pair_rows, width), BF16),
            pltpu.VMEM((NZ - 1, pair_rows, width), BF16),
            pltpu.VMEM((NZ - 1, pair_rows, width), BF16),
            pltpu.VMEM((NE, pair_rows, feat), BF16),
            pltpu.VMEM((NE, NT, pair_rows, feat), BF16),
            dma((TB,)), dma((2 * NT,)), dma((NG,)), dma((2,)),
            dma((NE - 1,)), dma((NE - 1,)),
            dma((NG,)), dma((NG,)),
            dma((NG, NT - 1)), dma((NG, NT - 1)),
            dma((NG,)), dma((NG,)),
            dma((NG, NZ - 1)), dma((NG, NZ - 1)),
            dma((NG, NZ - 1)), dma((NG, NZ - 1)),
            dma((NG, NZ)), dma((NG, NZ)),
            dma((NZ,)), dma((NZ,)),
            dma((NZ - 1,)), dma((NZ - 1,)),
            dma((NE - 1,)), dma((NE - 1,)),
        ],
        compiler_params=pltpu.CompilerParams(collective_id=0, has_side_effects=True, vmem_limit_bytes=60 << 20),
        name="dispatch_experts",
    )(tokens, slot_params.T, w_in, w_out)
    return pl.pallas_call(
        combine_kernel,
        out_shape=jax.ShapeDtypeStruct((seqs, length, feat), BF16),
        in_specs=[any_spec, pl.BlockSpec(memory_space=pltpu.VMEM)],
        out_specs=any_spec,
        scratch_shapes=[
            pltpu.VMEM((seqs, length, slots), BF16),
            pltpu.VMEM((NG, NE * NT * span, feat), BF16),
            pltpu.VMEM((seqs, length, feat), BF16),
            dma((NG,)), dma((seqs // 2,)),
        ],
        compiler_params=pltpu.CompilerParams(vmem_limit_bytes=60 << 20),
        name="combine",
    )(cw, g.reshape(NE * NT, pair_rows, feat))


def shards(tokens, slot_params, w_in, w_out):
    own_width = slot_params.shape[1]
    own_logits = jnp.einsum("std,dj->sjt", tokens, slot_params, preferred_element_type=jnp.float32)
    all_logits = lax.all_gather(own_logits, "exp", axis=1, tiled=True)
    local_max = jnp.max(own_logits, axis=2)
    slot_peak = lax.pmax(local_max, "tok")
    dexp = jnp.exp(own_logits - slot_peak[:, :, None])
    local_den = jnp.sum(dexp, axis=2)
    dweight = dexp.astype(jnp.bfloat16)
    local_sum = jnp.einsum("sjt,std->sjd", dweight, tokens, preferred_element_type=jnp.float32)
    slot_sum, slot_den = lax.psum((local_sum, local_den), "tok")
    slot_in = (slot_sum / slot_den[:, :, None]).astype(jnp.bfloat16)
    seq_count = tokens.shape[0]
    local_experts = w_in.shape[0]
    width = tokens.shape[2]
    grouped = slot_in.reshape(seq_count, local_experts, SLOTS_PER, width)
    hidden = jax.nn.gelu(
        jnp.einsum("sepd,edf->sepf", grouped, w_in, preferred_element_type=jnp.float32),
        approximate=True,
    ).astype(jnp.bfloat16)
    partial_out = jnp.einsum("sepf,efd->sepd", hidden, w_out, preferred_element_type=jnp.float32)
    partial_out = partial_out.reshape(seq_count, own_width, width)
    summed = lax.psum(partial_out, "tok").astype(jnp.bfloat16)
    slot_out = lax.all_to_all(summed, "exp", split_axis=2, concat_axis=1, tiled=True)
    comb_max = jnp.max(all_logits, axis=1)
    cexp = jnp.exp(all_logits - comb_max[:, None, :])
    cweight = (cexp / jnp.sum(cexp, axis=1)[:, None, :]).astype(jnp.bfloat16)
    mixed = jnp.einsum("sjt,sjd->std", cweight, slot_out, preferred_element_type=jnp.float32)
    return mixed.astype(jnp.bfloat16)


def solution(mesh):
    quick = mesh.shape["tok"] == NT and mesh.shape["exp"] == NE
    return jax.shard_map(
        fused if quick else shards,
        mesh=mesh,
        in_specs=(
            P(None, "tok", None),
            P(None, "exp"),
            P("exp", None, "tok"),
            P("exp", "tok", None),
        ),
        out_specs=P(None, "tok", "exp"),
        check_vma=False,
    )
```
